256 devices in a mesh: prefix: 8 (over x, core), sample: 32 (over y, z).
Axes of the slice: x: 4, y: 4, z: 8, core: 2. Of those that a mesh axis runs over, the one named last changes fastest.
Arguments:
- hidden_states: bfloat16 [128, 8192], P(None, 'sample'), may hold values from -400 to 400
- query_weight: bfloat16 [8192, 8192], P('sample', 'prefix'), may hold values from -0.044194174 to 0.044194174
- prefix_levels: bfloat16 [2, 4096, 8, 128], P(None, 'prefix'), may hold values from -127 to 127, as said below
- prefix_scale: float32 [2, 32, 8], P(None, 'prefix'), may hold values from 0.004 to 1
- suffix_cache: bfloat16 [2, 128, 4096, 8, 128], P(None, 'sample', 'prefix'), may hold values from -12 to 12
- lengths: int32 [128], P('sample'), may hold values from 1 to 4096, 262144 in all
- output_weight: bfloat16 [8192, 8192], P('prefix', 'sample'), may hold values from -0.0625 to 0.0625
Outputs:
- mixed: bfloat16 [128, 8192], P('prefix', 'sample')
The draws below stay inside these ranges and needn't reach their ends.
Inputs may be any that keep to these rules, and one draw needn't show every extreme that they name: Sample b's suffix cache is live at positions below lengths[b]; some sample has exactly 4096. `prefix_levels`: whole numbers.
All inputs are finite; a program needn't handle non-finite values. No bound on the sum of `lengths` on one device may be relied on, other than what follows from the above.
Results may differ from the reference program's by a relative error of at most 0.02.
Values may be sent and summed in bfloat16 or wider, within the bound.
A program may use at most 64 MiB of HBM per device.

```python
import math
import jax
import jax.numpy as jnp
import numpy as np
from jax import lax

D = 8192
H = 64
KV = 8
HD = 128
BLOCK = 128
SUFFIX = 4096
SAMPLES = 128
PREFIX = 4096
NBLK = 32


def scaled_rows(key):
    seeded = jax.random.fold_in(key, 11)
    key_row, key_column, key_entries = jax.random.split(seeded, 3)
    row_scale = jnp.exp(jax.random.uniform(key_row, (SAMPLES, 1), jnp.float32, 0.0, math.log(10.0)))
    rising = jnp.exp(math.log(3.0) * jnp.arange(D, dtype=jnp.float32) / D)
    column_scale = jnp.exp(jax.random.uniform(key_column, (1, D), jnp.float32, 0.0, math.log(3.16))) * rising[None, :]
    entries = jax.random.truncated_normal(key_entries, -4.0, 4.0, (SAMPLES, D), jnp.float32)
    return entries * row_scale * column_scale


def head_columns(key, number):
    seeded = jax.random.fold_in(jax.random.fold_in(key, 12), number)
    return jax.random.truncated_normal(seeded, -4.0, 4.0, (D, HD), jnp.float32) / math.sqrt(D)


def cache_levels(key):
    levels = jax.random.randint(jax.random.fold_in(key, 13), (2, PREFIX, KV, HD), -127, 128).astype(jnp.float32)
    scales = jnp.exp(jax.random.uniform(jax.random.fold_in(key, 14), (2, NBLK, KV), jnp.float32, math.log(0.004), math.log(0.04)))
    return (levels, scales)


def draw_hidden_states(key, part):
    return scaled_rows(key).astype(jnp.bfloat16)


def draw_query_weight(key, part):

    def per_head(number):
        return head_columns(key, number)
    stacked = jax.vmap(per_head)(jnp.arange(H, dtype=jnp.int32))
    return jnp.transpose(stacked, (1, 0, 2)).reshape(D, H * HD).astype(jnp.bfloat16)


def draw_prefix_levels(key, part):
    return cache_levels(key)[0].astype(jnp.bfloat16)


def draw_prefix_scale(key, part):
    return cache_levels(key)[1]


def block_levels(key, dims, cuts, smallest, top_value):
    level, own = 1.0, jax.random.fold_in(key, 6)
    for dim, blocks in cuts:
        steps = jnp.exp(jax.random.uniform(jax.random.fold_in(own, dim), (blocks,), jnp.float32, smallest / len(cuts), top_value / len(cuts)))
        level = level * jnp.repeat(steps, dims[dim] // blocks).reshape([-1 if axis == dim else 1 for axis in range(len(dims))])
    return level


def length_profile(amount, total, most, slope):
    portions = [(1 << 20) // math.isqrt(rank ** slope) + 1 for rank in range(2, amount + 1)]
    rest, holding = total - most - (amount - 1), [1] * (amount - 1)
    while rest > 0:
        movable = [i for i in range(amount - 1) if holding[i] < most]
        whole, budget = sum([portions[i] for i in movable]), rest
        for i in movable:
            more = min(most - holding[i], max(1, budget * portions[i] // whole), rest)
            holding[i] = holding[i] + more
            rest = rest - more
    return np.array([most] + holding)


def ragged_sizes(key, number_of, total, reach, skew):
    if number_of == 2:
        one = jax.random.randint(key, (), max(1, total - reach), min(reach, total - 1) + 1)
        return jnp.stack([one, total - one])
    tallies = jnp.asarray(length_profile(number_of, total, reach, skew), jnp.int32)
    twos = (number_of - 1) // 2
    giver, receiver = tallies[1:1 + 2 * twos:2], tallies[2:2 + 2 * twos:2]
    room = jnp.minimum(giver - 1, reach - receiver)
    shifted = jax.random.randint(jax.random.fold_in(key, 1), (twos,), 0, 1 << 20) % (room + 1)
    tallies = tallies.at[1:1 + 2 * twos:2].set(giver - shifted).at[2:2 + 2 * twos:2].set(receiver + shifted)
    return tallies[jax.random.permutation(jax.random.fold_in(key, 2), number_of)]


def scatter_about(rng, extent, deviation, limit, pieces=(), kind=jnp.bfloat16):
    values = jax.random.normal(rng, extent, jnp.float32) * deviation
    if len(pieces) > 0:
        values = block_levels(rng, extent, pieces, -0.22, 0.18) * values
    return jnp.clip(values, min=-limit, max=limit).astype(kind)


def setup_inputs(seed: int = 0) -> dict:
    keys = jax.random.split(jax.random.key(seed), 8)
    return {
        "hidden_states": draw_hidden_states(jax.random.fold_in(keys[7], 71), 0),
        "query_weight": draw_query_weight(jax.random.fold_in(keys[7], 71), 0),
        "prefix_levels": draw_prefix_levels(jax.random.fold_in(keys[7], 71), 0),
        "prefix_scale": draw_prefix_scale(jax.random.fold_in(keys[7], 71), 0),
        "suffix_cache": scatter_about(keys[4], (2, SAMPLES, SUFFIX, KV, HD), 2.0, 12.0, ((1, 32), (2, 8))),
        "lengths": ragged_sizes(keys[5], SAMPLES, SAMPLES * SUFFIX // 2, SUFFIX, 2).astype(jnp.int32),
        "output_weight": scatter_about(keys[6], (H * HD, D), (H * HD) ** -0.5, 0.0625, ((0, 8), (1, 32))),
    }


def reference(hidden_states, query_weight, prefix_levels, prefix_scale, suffix_cache, lengths, output_weight):
    state_float = hidden_states.astype(jnp.float32)
    mean_sq = lax.optimization_barrier(jnp.mean(state_float * state_float, axis=1, keepdims=True))
    queries = (jnp.dot(hidden_states, query_weight, preferred_element_type=jnp.float32) * lax.rsqrt(mean_sq + 1e-05)).astype(jnp.bfloat16)
    per_group = H // KV
    grouped = queries.reshape(SAMPLES, KV, per_group, HD)
    scaling = 1.0 / math.sqrt(HD)
    live_mask = jnp.arange(SUFFIX, dtype=jnp.int32)[None, :] < lengths[:, None]

    def attend_group(group_index):
        query_group = lax.dynamic_index_in_dim(grouped, group_index, 1, False).astype(jnp.float32)
        key_level = lax.dynamic_index_in_dim(prefix_levels[0], group_index, 1, False).astype(jnp.float32)
        value_level = lax.dynamic_index_in_dim(prefix_levels[1], group_index, 1, False).astype(jnp.float32)
        key_scale = jnp.repeat(lax.dynamic_index_in_dim(prefix_scale[0], group_index, 1, False), BLOCK)
        value_scale = jnp.repeat(lax.dynamic_index_in_dim(prefix_scale[1], group_index, 1, False), BLOCK)
        suffix_keys = lax.dynamic_index_in_dim(suffix_cache[0], group_index, 2, False).astype(jnp.float32)
        suffix_values = lax.dynamic_index_in_dim(suffix_cache[1], group_index, 2, False).astype(jnp.float32)
        prefix_scores = jnp.einsum('brd,td->brt', query_group, key_level) * key_scale[None, None, :] * scaling
        suffix_scores = jnp.einsum('brd,btd->brt', query_group, suffix_keys) * scaling
        suffix_scores = jnp.where(live_mask[:, None, :], suffix_scores, -jnp.inf)
        top_score = jnp.maximum(lax.optimization_barrier(jnp.max(prefix_scores, axis=2)), lax.optimization_barrier(jnp.max(suffix_scores, axis=2)))
        prefix_exp = jnp.exp(prefix_scores - top_score[:, :, None])
        suffix_exp = jnp.exp(suffix_scores - top_score[:, :, None])
        denominator = lax.optimization_barrier(jnp.sum(prefix_exp, axis=2)) + lax.optimization_barrier(jnp.sum(suffix_exp, axis=2))
        prefix_weights = (prefix_exp * value_scale[None, None, :]).astype(jnp.bfloat16).astype(jnp.float32)
        suffix_weights = suffix_exp.astype(jnp.bfloat16).astype(jnp.float32)
        combined = jnp.einsum('brt,td->brd', prefix_weights, value_level) + jnp.einsum('brt,btd->brd', suffix_weights, suffix_values)
        return combined / denominator[:, :, None]
    outputs = lax.map(attend_group, jnp.arange(KV, dtype=jnp.int32))
    attended = jnp.transpose(outputs, (1, 0, 2, 3)).reshape(SAMPLES, H * HD).astype(jnp.bfloat16)
    return jnp.dot(attended, output_weight, preferred_element_type=jnp.float32).astype(jnp.bfloat16)
```

```python
import functools
import math

import jax
import jax.numpy as jnp
from jax import lax
from jax.experimental import pallas as pl
from jax.experimental.pallas import tpu as pltpu
from jax.sharding import PartitionSpec as P

MESH = pl.DeviceIdType.MESH
EPSILON = 1e-05
BLOCK = 128
NX, NC, NY, NZ = 4, 2, 4, 8
NP = NX * NC
OWN = 4
HD = 128
GROUPS = 8
REP = 8
ROWS = OWN * REP
COLS = REP * HD
WIDE = COLS + 128
SPAN = 512
D = 8192
SCALING = 1.0 / math.sqrt(HD)
X_ORDER = (0, 1, 3, 2)
FAR_FIRST = (4, 3, 5, 2, 6, 1, 7, 0)
NEAR_FIRST = FAR_FIRST[::-1]
F32 = jnp.float32
BF16 = jnp.bfloat16


def split_lanes(values):
    folded = values + pltpu.roll(values, 64, 1)
    high = folded.astype(BF16).astype(F32)
    lane = lax.broadcasted_iota(jnp.int32, folded.shape, 1)
    return jnp.where(lane < 64, high, folded - high)


def regroup(source, target):
    tokens = 64

    @pl.loop(0, SPAN // tokens)
    def _(step):
        rows = source[pl.ds(pl.multiple_of(step * tokens * GROUPS, tokens * GROUPS), tokens * GROUPS), :]
        rows = jnp.swapaxes(rows.reshape(tokens, GROUPS, HD), 0, 1)
        target[:, pl.ds(pl.multiple_of(step * tokens, tokens), tokens), :] = rows


def across(a, b):
    return lax.dot_general(a, b, (((1,), (1,)), ((), ())), preferred_element_type=F32)


def kernel(
    scale, lengths, hidden_hbm, wq_hbm, prefix_hbm, suffix_hbm, wo_hbm, out,
    hidden, wq, wo, praw, sraw, pre, suf, partial, ysend, yrecv, mine, zsend, zrecv, qrows, qall,
    csend, crecv, heads, osend, orecv,
    load_sem, raw_sem, ys, yr, zs, zr, qs, qr, cs, cr, gs, gr, hs, hr, os_, or_,
):
    p = lax.axis_index("prefix")
    s = lax.axis_index("sample")
    x, c = p // NC, p % NC
    y, z = s // NZ, s % NZ

    def at_y(k):
        return (p, lax.rem(y + k, NY) * NZ + z)

    def at_z(k):
        return (p, y * NZ + lax.rem(z + k, NZ))

    def prefix_of(dx, dc):
        return lax.rem(x + dx, NX) * NC + lax.rem(c + dc, NC)

    def remote(src, dst, ssem, rsem, device):
        return pltpu.make_async_remote_copy(
            src_ref=src, dst_ref=dst, send_sem=ssem, recv_sem=rsem, device_id=device, device_id_type=MESH
        )

    pending = []

    def start(copy):
        copy.start()
        pending.append(copy)
        return copy

    others = [(dx, dc) for dx in X_ORDER for dc in range(NC) if dx or dc]

    load_hidden = pltpu.make_async_copy(hidden_hbm, hidden, load_sem.at[0])
    load_wq = pltpu.make_async_copy(wq_hbm, wq, load_sem.at[1])
    load_wo = pltpu.make_async_copy(wo_hbm, wo, load_sem.at[2])
    load_hidden.start()
    load_wq.start()

    barrier = pltpu.get_barrier_semaphore()
    for k in range(1, NZ):
        pl.semaphore_signal(barrier, inc=1, device_id=at_z(k), device_id_type=MESH)
    for k in range(1, NY):
        pl.semaphore_signal(barrier, inc=1, device_id=at_y(k), device_id_type=MESH)
    for dx, dc in others:
        pl.semaphore_signal(barrier, inc=1, device_id=(prefix_of(dx, dc), s), device_id_type=MESH)

    load_hidden.wait()
    load_wq.wait()

    raw = []
    for side in range(2):
        for i in range(OWN):
            raw.append(
                (
                    pltpu.make_async_copy(suffix_hbm.at[side, i], sraw.at[side, i], raw_sem.at[side, i]),
                    sraw.at[side, i],
                    suf.at[side, i],
                )
            )
        raw.append(
            (
                pltpu.make_async_copy(prefix_hbm.at[side], praw.at[side], raw_sem.at[side, OWN]),
                praw.at[side],
                pre.at[side],
            )
        )
    for copy, _, _ in raw:
        copy.start()
    load_wo.start()

    wide = 256
    for n in range(COLS // wide):
        cols = pl.ds(n * wide, wide)
        partial[:, cols] = jnp.dot(hidden[...], wq[:, cols], preferred_element_type=F32)
    values = hidden[...].astype(F32)
    values = values * values
    partial[:, COLS:] = split_lanes(values[:, :128] + values[:, 128:])

    pl.semaphore_wait(barrier, NZ - 1 + NY - 1 + NP - 1)

    for k in range(1, NY):
        first = pl.multiple_of(lax.rem(y + k, NY) * NZ * OWN, NZ * OWN)
        block = partial[pl.ds(first, NZ * OWN), :].astype(BF16)
        for j in range(NZ):
            ysend[k - 1, j] = block[OWN * j : OWN * (j + 1)]
    ycopies = []
    for n in FAR_FIRST:
        slot = lax.rem(z + n, NZ)
        for k in (2, 1, 3):
            copy = remote(
                ysend.at[k - 1, slot], yrecv.at[k - 1, n], ys.at[k - 1, n], yr.at[k - 1, n], at_y(k)
            )
            ycopies.append(start(copy))
    first = pl.multiple_of(y * NZ * OWN, NZ * OWN)
    block = partial[pl.ds(first, NZ * OWN), :]
    for j in range(NZ):
        mine[j] = block[OWN * j : OWN * (j + 1)]

    for copy, source, target in raw[: OWN + 1]:
        copy.wait()
        regroup(source, target)
    zcopies = []
    for m, n in enumerate(FAR_FIRST):
        slot = lax.rem(z + n, NZ)
        summed = mine[slot]
        for i, k in enumerate((2, 1, 3)):
            ycopies[(NY - 1) * m + i].wait_recv()
            summed = summed + yrecv[k - 1, n].astype(F32)
        if n == 0:
            mine[slot] = summed
            break
        zsend[n - 1, :, :COLS] = summed[:, :COLS].astype(BF16)
        zsend[n - 1, :, COLS:] = split_lanes(summed[:, COLS:]).astype(BF16)
        copy = remote(zsend.at[n - 1], zrecv.at[n - 1], zs.at[n - 1], zr.at[n - 1], at_z(n))
        zcopies.append(start(copy))
    for copy, source, target in raw[OWN + 1 :]:
        copy.wait()
        regroup(source, target)
    for copy in zcopies:
        copy.wait_recv()
    own = mine[z]
    for k in range(1, NZ):
        own = own + zrecv[k - 1].astype(F32)
    mean_sq = jnp.sum(own[:, COLS:], axis=1, keepdims=True) * (1.0 / D)
    scaled = own[:, :COLS] * lax.rsqrt(mean_sq + EPSILON)
    for r in range(REP):
        qrows[OWN * r : OWN * (r + 1), :] = scaled[:, HD * r : HD * (r + 1)]
    qall[p] = jnp.concatenate(
        [qrows[pl.ds(i, REP, stride=OWN), :] for i in range(OWN)], axis=0
    ).astype(BF16)
    for k, (dx, dc) in enumerate(others[::-1]):
        copy = remote(qall.at[p], qall.at[p], qs.at[k], qr.at[p], (prefix_of(dx, dc), s))
        start(copy)

    first_position = p * SPAN
    place = lax.broadcasted_iota(jnp.int32, (REP, SPAN), 1) + first_position
    live = [place < lengths[i] for i in range(OWN)]
    row_id = lax.broadcasted_iota(jnp.int32, (ROWS, 128), 0)
    lane_id = lax.broadcasted_iota(jnp.int32, (ROWS, 128), 1)
    diagonal = row_id == lane_id
    top_row = lax.broadcasted_iota(jnp.int32, (8, 128), 0) == 0

    def attend(g):
        q = qall[g]
        raw_scores = across(q, pre[0, g])
        prefix_scores = jnp.concatenate(
            [
                raw_scores[:, BLOCK * b : BLOCK * (b + 1)] * (scale[0, b, g] * SCALING)
                for b in range(SPAN // BLOCK)
            ],
            axis=1,
        )
        pieces = []
        for i in range(OWN):
            pair = q[16 * (i // 2) : 16 * (i // 2 + 1)]
            score = across(pair, suf[0, i, g])[8 * (i % 2) : 8 * (i % 2) + 8] * SCALING
            pieces.append(jnp.where(live[i], score, -jnp.inf))
        suffix_scores = jnp.concatenate(pieces, axis=0)
        peak = jnp.maximum(
            jnp.max(prefix_scores, axis=1, keepdims=True), jnp.max(suffix_scores, axis=1, keepdims=True)
        )
        prefix_exp = jnp.exp(prefix_scores - peak)
        suffix_exp = jnp.exp(suffix_scores - peak)
        total = jnp.sum(prefix_exp, axis=1, keepdims=True) + jnp.sum(suffix_exp, axis=1, keepdims=True)
        prefix_weights = jnp.concatenate(
            [
                prefix_exp[:, BLOCK * b : BLOCK * (b + 1)] * scale[1, b, g]
                for b in range(SPAN // BLOCK)
            ],
            axis=1,
        ).astype(BF16)
        suffix_weights = suffix_exp.astype(BF16)
        weighted = jnp.dot(prefix_weights, pre[1, g], preferred_element_type=F32)
        pieces = []
        for i in range(OWN):
            pair = suffix_weights[16 * (i // 2) : 16 * (i // 2 + 1)]
            value = jnp.dot(pair, suf[1, i, g], preferred_element_type=F32)
            pieces.append(value[8 * (i % 2) : 8 * (i % 2) + 8])
        csend[g, :ROWS] = weighted + jnp.concatenate(pieces, axis=0)
        peak_row = jnp.sum(jnp.where(diagonal, peak, 0.0), axis=0, keepdims=True)
        total_row = jnp.sum(jnp.where(diagonal, total, 0.0), axis=0, keepdims=True)
        csend[g, ROWS:] = jnp.where(top_row, peak_row, total_row)

    for dx in X_ORDER:
        for dc in range(NC):
            if dx or dc:
                g = prefix_of(dx, dc)
                remote(qall.at[g], qall.at[g], qs.at[0], qr.at[g], (g, s)).wait_recv()
        for dc in range(NC):
            attend(prefix_of(dx, dc))
        for dc in range(NC):
            if dx or dc:
                g = prefix_of(dx, dc)
                start(remote(csend.at[g], crecv.at[p], cs.at[g], cr.at[p], (g, s)))

    for dx, dc in others:
        g = prefix_of(dx, dc)
        remote(csend.at[g], crecv.at[g], cs.at[g], cr.at[g], (g, s)).wait_recv()

    parts = [csend[p]] + [crecv[prefix_of(dx, dc)] for dx, dc in others]
    peaks = [part[ROWS : ROWS + 1] for part in parts]
    totals = [part[ROWS + 1 : ROWS + 2] for part in parts]
    top = functools.reduce(jnp.maximum, peaks)
    factors = [jnp.exp(peak - top) for peak in peaks]
    whole = functools.reduce(jnp.add, [f * t for f, t in zip(factors, totals)])
    attended = None
    for part, factor in zip(parts, factors):
        share = jnp.sum(jnp.where(diagonal, factor / whole, 0.0), axis=1, keepdims=True)
        term = part[:ROWS] * share
        attended = term if attended is None else attended + term
    heads[y, z] = attended.astype(BF16)
    for k in FAR_FIRST[:-1]:
        start(remote(heads.at[y, z], heads.at[y, z], gs.at[k - 1], gr.at[z], at_z(k)))
    load_wo.wait()
    for n in NEAR_FIRST:
        slot = lax.rem(z + n, NZ)
        if n:
            remote(heads.at[y, slot], heads.at[y, slot], gs.at[n - 1], gr.at[slot], at_z(n)).wait_recv()
        for k in (2, 1, 3):
            start(
                remote(
                    heads.at[y, slot], heads.at[y, slot], hs.at[k - 1, slot], hr.at[y, slot], at_y(k)
                )
            )
    for k in (0, 1, 3, 2):
        block = lax.rem(y + k, NY)
        if k:
            for j in range(NZ):
                remote(
                    heads.at[block, j], heads.at[block, j], hs.at[k - 1, j], hr.at[block, j], at_y(k)
                ).wait_recv()
        rows = jnp.swapaxes(heads[block].reshape(NZ * OWN, REP, HD), 0, 1)
        rows = jnp.concatenate([rows[r] for r in range(REP)], axis=1)
        product = jnp.dot(rows, wo[...], preferred_element_type=F32).astype(BF16)
        for half in range(2):
            g = block * 2 + half
            osend[g] = product[16 * half : 16 * (half + 1)]

            @pl.when(g != p)
            def _():
                remote(osend.at[g], orecv.at[p], os_.at[g], or_.at[p], (g, s)).start()

    for dx, dc in others:
        g = prefix_of(dx, dc)
        remote(osend.at[g], orecv.at[g], os_.at[g], or_.at[g], (g, s)).wait_recv()
    result = osend[p].astype(F32)
    for dx, dc in others:
        result = result + orecv[prefix_of(dx, dc)].astype(F32)
    out[...] = result.astype(BF16)

    for copy in pending:
        copy.wait_send()
    for dx, dc in others:
        g = prefix_of(dx, dc)
        remote(osend.at[g], orecv.at[p], os_.at[g], or_.at[p], (g, s)).wait_send()


def on_device(
    hidden_states, query_weight, prefix_levels, prefix_scale, suffix_cache, lengths, output_weight
):
    anywhere = pl.BlockSpec(memory_space=pl.ANY)
    scalar = pl.BlockSpec(memory_space=pltpu.SMEM)
    dma = pltpu.SemaphoreType.DMA
    call = pl.pallas_call(
        kernel,
        out_shape=jax.ShapeDtypeStruct((16, 256), BF16),
        in_specs=[scalar, scalar] + [anywhere] * 5,
        out_specs=pl.BlockSpec(memory_space=pltpu.VMEM),
        scratch_shapes=[
            pltpu.VMEM((128, 256), BF16),
            pltpu.VMEM((256, COLS), BF16),
            pltpu.VMEM((COLS, 256), BF16),
            pltpu.VMEM((2, SPAN * GROUPS, HD), BF16),
            pltpu.VMEM((2, OWN, SPAN * GROUPS, HD), BF16),
            pltpu.VMEM((2, GROUPS, SPAN, HD), BF16),
            pltpu.VMEM((2, OWN, GROUPS, SPAN, HD), BF16),
            pltpu.VMEM((128, WIDE), F32),
            pltpu.VMEM((NY - 1, NZ, OWN, WIDE), BF16),
            pltpu.VMEM((NY - 1, NZ, OWN, WIDE), BF16),
            pltpu.VMEM((NZ, OWN, WIDE), F32),
            pltpu.VMEM((NZ - 1, OWN, WIDE), BF16),
            pltpu.VMEM((NZ - 1, OWN, WIDE), BF16),
            pltpu.VMEM((ROWS, HD), F32),
            pltpu.VMEM((NP, ROWS, HD), BF16),
            pltpu.VMEM((NP, ROWS + 8, HD), F32),
            pltpu.VMEM((NP, ROWS + 8, HD), F32),
            pltpu.VMEM((NY, NZ, ROWS, HD), BF16),
            pltpu.VMEM((NP, 16, 256), BF16),
            pltpu.VMEM((NP, 16, 256), BF16),
            dma((3,)),
            dma((2, OWN + 1)),
            dma((NY - 1, NZ)),
            dma((NY - 1, NZ)),
            dma((NZ - 1,)),
            dma((NZ - 1,)),
            dma((NP - 1,)),
            dma((NP,)),
            dma((NP,)),
            dma((NP,)),
            dma((NZ - 1,)),
            dma((NZ,)),
            dma((NY - 1, NZ)),
            dma((NY, NZ)),
            dma((NP,)),
            dma((NP,)),
        ],
        compiler_params=pltpu.CompilerParams(
            collective_id=0, has_side_effects=True, vmem_limit_bytes=60 * 2**20
        ),
        name="layer",
    )
    return call(
        prefix_scale,
        lengths,
        hidden_states,
        query_weight,
        prefix_levels.reshape(2, SPAN * GROUPS, HD),
        suffix_cache.reshape(2, OWN, SPAN * GROUPS, HD),
        output_weight,
    )


def solution(mesh):
    return jax.shard_map(
        on_device,
        mesh=mesh,
        in_specs=(
            P(None, "sample"),
            P("sample", "prefix"),
            P(None, "prefix", None, None),
            P(None, "prefix", None),
            P(None, "sample", "prefix", None, None),
            P("sample"),
            P("prefix", "sample"),
        ),
        out_specs=P("prefix", "sample"),
        check_vma=False,
    )
```

```python
import functools
import math

import jax
import jax.numpy as jnp
from jax import lax
from jax.experimental import pallas as pl
from jax.experimental.pallas import tpu as pltpu
from jax.sharding import PartitionSpec as P

MESH = pl.DeviceIdType.MESH
EPSILON = 1e-05
BLOCK = 128
NX, NC, NY, NZ = 4, 2, 4, 8
NP = NX * NC
OWN = 4
HD = 128
GROUPS = 8
REP = 8
ROWS = OWN * REP
COLS = REP * HD
WIDE = COLS + 128
SPAN = 512
D = 8192
SCALING = 1.0 / math.sqrt(HD)
X_ORDER = (0, 1, 3, 2)
FAR_FIRST = (4, 3, 5, 2, 6, 1, 7, 0)
NEAR_FIRST = FAR_FIRST[::-1]
F32 = jnp.float32
BF16 = jnp.bfloat16


def split_lanes(values):
    folded = values + pltpu.roll(values, 64, 1)
    high = folded.astype(BF16).astype(F32)
    lane = lax.broadcasted_iota(jnp.int32, folded.shape, 1)
    return jnp.where(lane < 64, high, folded - high)


def regroup(source, target):
    tokens = 64

    @pl.loop(0, SPAN // tokens)
    def _(step):
        rows = source[pl.ds(pl.multiple_of(step * tokens * GROUPS, tokens * GROUPS), tokens * GROUPS), :]
        rows = jnp.swapaxes(rows.reshape(tokens, GROUPS, HD), 0, 1)
        target[:, pl.ds(pl.multiple_of(step * tokens, tokens), tokens), :] = rows


def across(a, b):
    return lax.dot_general(a, b, (((1,), (1,)), ((), ())), preferred_element_type=F32)


def kernel(
    scale_hbm, lengths_hbm, hidden_hbm, wq_hbm, prefix_hbm, suffix_hbm, wo_hbm, out,
    hidden, wq, wo, praw, sraw, pre, suf, partial, ysend, yrecv, mine, zsend, zrecv, qrows, qall,
    csend, crecv, heads, osend, orecv,
    scale, lengths, ready, load_sem, raw_sem, ys, yr, zs, zr, qs, qr, cs, cr, gs, gr, hs, hr, os_, or_,
):
    p = lax.axis_index("prefix")
    s = lax.axis_index("sample")
    x, c = p // NC, p % NC
    y, z = s // NZ, s % NZ

    def at_y(k):
        return (p, lax.rem(y + k, NY) * NZ + z)

    def at_z(k):
        return (p, y * NZ + lax.rem(z + k, NZ))

    def prefix_of(dx, dc):
        return lax.rem(x + dx, NX) * NC + lax.rem(c + dc, NC)

    def remote(src, dst, ssem, rsem, device):
        return pltpu.make_async_remote_copy(
            src_ref=src, dst_ref=dst, send_sem=ssem, recv_sem=rsem, device_id=device, device_id_type=MESH
        )

    pending = []

    def start(copy):
        copy.start()
        pending.append(copy)
        return copy

    others = [(dx, dc) for dx in X_ORDER for dc in range(NC) if dx or dc]

    load_hidden = pltpu.make_async_copy(hidden_hbm, hidden, load_sem.at[0])
    load_wq = pltpu.make_async_copy(wq_hbm, wq, load_sem.at[1])
    load_wo = pltpu.make_async_copy(wo_hbm, wo, load_sem.at[2])
    load_scale = pltpu.make_async_copy(scale_hbm, scale, load_sem.at[3])
    load_lengths = pltpu.make_async_copy(lengths_hbm, lengths, load_sem.at[4])
    load_hidden.start()
    load_wq.start()
    load_scale.start()
    load_lengths.start()

    barrier = pltpu.get_barrier_semaphore()
    for k in (1, NZ - 1):
        pl.semaphore_signal(barrier, inc=1, device_id=at_z(k), device_id_type=MESH)
    for k in range(1, NY):
        pl.semaphore_signal(barrier, inc=1, device_id=at_y(k), device_id_type=MESH)
    for dx, dc in others:
        pl.semaphore_signal(barrier, inc=1, device_id=(prefix_of(dx, dc), s), device_id_type=MESH)

    load_hidden.wait()
    load_wq.wait()

    raw = []
    for side in range(2):
        for i in range(OWN):
            raw.append(
                (
                    pltpu.make_async_copy(suffix_hbm.at[side, i], sraw.at[side, i], raw_sem.at[side, i]),
                    sraw.at[side, i],
                    suf.at[side, i],
                )
            )
        raw.append(
            (
                pltpu.make_async_copy(prefix_hbm.at[side], praw.at[side], raw_sem.at[side, OWN]),
                praw.at[side],
                pre.at[side],
            )
        )
    for copy, _, _ in raw:
        copy.start()
    load_wo.start()

    wide = 256
    for n in range(COLS // wide):
        cols = pl.ds(n * wide, wide)
        partial[:, cols] = jnp.dot(hidden[...], wq[:, cols], preferred_element_type=F32)
    values = hidden[...].astype(F32)
    values = values * values
    partial[:, COLS:] = split_lanes(values[:, :128] + values[:, 128:])

    pl.semaphore_wait(barrier, 2 + NY - 1 + NP - 1)
    for k in (1, NZ - 1):
        pl.semaphore_signal(ready.at[0], inc=1, device_id=at_z(k), device_id_type=MESH)

    for k in range(1, NY):
        first = pl.multiple_of(lax.rem(y + k, NY) * NZ * OWN, NZ * OWN)
        block = partial[pl.ds(first, NZ * OWN), :].astype(BF16)
        for j in range(NZ):
            ysend[k - 1, j] = block[OWN * j : OWN * (j + 1)]
    ycopies = []
    for n in FAR_FIRST:
        slot = lax.rem(z + n, NZ)
        for k in (2, 1, 3):
            copy = remote(
                ysend.at[k - 1, slot], yrecv.at[k - 1, n], ys.at[k - 1, n], yr.at[k - 1, n], at_y(k)
            )
            ycopies.append(start(copy))
    first = pl.multiple_of(y * NZ * OWN, NZ * OWN)
    block = partial[pl.ds(first, NZ * OWN), :]
    for j in range(NZ):
        mine[j] = block[OWN * j : OWN * (j + 1)]

    for n, (copy, source, target) in enumerate(raw[: OWN + 1]):
        copy.wait()
        regroup(source, target)
        if n == 1:
            pl.semaphore_wait(ready.at[0], 2)
            for k in (2, NZ - 2):
                pl.semaphore_signal(ready.at[1], inc=1, device_id=at_z(k), device_id_type=MESH)
    pl.semaphore_wait(ready.at[1], 2)
    zcopies = []
    for m, n in enumerate(FAR_FIRST):
        slot = lax.rem(z + n, NZ)
        summed = mine[slot]
        for i, k in enumerate((2, 1, 3)):
            ycopies[(NY - 1) * m + i].wait_recv()
            summed = summed + yrecv[k - 1, n].astype(F32)
        if n == 0:
            mine[slot] = summed
            break
        zsend[n - 1, :, :COLS] = summed[:, :COLS].astype(BF16)
        zsend[n - 1, :, COLS:] = split_lanes(summed[:, COLS:]).astype(BF16)
        copy = remote(zsend.at[n - 1], zrecv.at[n - 1], zs.at[n - 1], zr.at[n - 1], at_z(n))
        zcopies.append(start(copy))
    for copy, source, target in raw[OWN + 1 :]:
        copy.wait()
        regroup(source, target)
    for copy in zcopies:
        copy.wait_recv()
    own = mine[z]
    for k in range(1, NZ):
        own = own + zrecv[k - 1].astype(F32)
    mean_sq = jnp.sum(own[:, COLS:], axis=1, keepdims=True) * (1.0 / D)
    scaled = own[:, :COLS] * lax.rsqrt(mean_sq + EPSILON)
    for r in range(REP):
        qrows[OWN * r : OWN * (r + 1), :] = scaled[:, HD * r : HD * (r + 1)]
    qall[p] = jnp.concatenate(
        [qrows[pl.ds(i, REP, stride=OWN), :] for i in range(OWN)], axis=0
    ).astype(BF16)
    for k, (dx, dc) in enumerate(others[::-1]):
        copy = remote(qall.at[p], qall.at[p], qs.at[k], qr.at[p], (prefix_of(dx, dc), s))
        start(copy)

    load_scale.wait()
    load_lengths.wait()
    first_position = p * SPAN
    place = lax.broadcasted_iota(jnp.int32, (REP, SPAN), 1) + first_position
    live = [place < lengths[i] for i in range(OWN)]
    row_id = lax.broadcasted_iota(jnp.int32, (ROWS, 128), 0)
    lane_id = lax.broadcasted_iota(jnp.int32, (ROWS, 128), 1)
    diagonal = row_id == lane_id
    top_row = lax.broadcasted_iota(jnp.int32, (8, 128), 0) == 0

    def attend(g):
        q = qall[g]
        raw_scores = across(q, pre[0, g])
        prefix_scores = jnp.concatenate(
            [
                raw_scores[:, BLOCK * b : BLOCK * (b + 1)] * (scale[0, b, g] * SCALING)
                for b in range(SPAN // BLOCK)
            ],
            axis=1,
        )
        pieces = []
        for i in range(OWN):
            pair = q[16 * (i // 2) : 16 * (i // 2 + 1)]
            score = across(pair, suf[0, i, g])[8 * (i % 2) : 8 * (i % 2) + 8] * SCALING
            pieces.append(jnp.where(live[i], score, -jnp.inf))
        suffix_scores = jnp.concatenate(pieces, axis=0)
        peak = jnp.maximum(
            jnp.max(prefix_scores, axis=1, keepdims=True), jnp.max(suffix_scores, axis=1, keepdims=True)
        )
        prefix_exp = jnp.exp(prefix_scores - peak)
        suffix_exp = jnp.exp(suffix_scores - peak)
        total = jnp.sum(prefix_exp, axis=1, keepdims=True) + jnp.sum(suffix_exp, axis=1, keepdims=True)
        prefix_weights = jnp.concatenate(
            [
                prefix_exp[:, BLOCK * b : BLOCK * (b + 1)] * scale[1, b, g]
                for b in range(SPAN // BLOCK)
            ],
            axis=1,
        ).astype(BF16)
        suffix_weights = suffix_exp.astype(BF16)
        weighted = jnp.dot(prefix_weights, pre[1, g], preferred_element_type=F32)
        pieces = []
        for i in range(OWN):
            pair = suffix_weights[16 * (i // 2) : 16 * (i // 2 + 1)]
            value = jnp.dot(pair, suf[1, i, g], preferred_element_type=F32)
            pieces.append(value[8 * (i % 2) : 8 * (i % 2) + 8])
        csend[g, :ROWS] = weighted + jnp.concatenate(pieces, axis=0)
        peak_row = jnp.sum(jnp.where(diagonal, peak, 0.0), axis=0, keepdims=True)
        total_row = jnp.sum(jnp.where(diagonal, total, 0.0), axis=0, keepdims=True)
        csend[g, ROWS:] = jnp.where(top_row, peak_row, total_row)

    for dx in X_ORDER:
        for dc in range(NC):
            if dx or dc:
                g = prefix_of(dx, dc)
                remote(qall.at[g], qall.at[g], qs.at[0], qr.at[g], (g, s)).wait_recv()
        for dc in range(NC):
            attend(prefix_of(dx, dc))
        for dc in range(NC):
            if dx or dc:
                g = prefix_of(dx, dc)
                start(remote(csend.at[g], crecv.at[p], cs.at[g], cr.at[p], (g, s)))

    for dx, dc in others:
        g = prefix_of(dx, dc)
        remote(csend.at[g], crecv.at[g], cs.at[g], cr.at[g], (g, s)).wait_recv()

    parts = [csend[p]] + [crecv[prefix_of(dx, dc)] for dx, dc in others]
    peaks = [part[ROWS : ROWS + 1] for part in parts]
    totals = [part[ROWS + 1 : ROWS + 2] for part in parts]
    top = functools.reduce(jnp.maximum, peaks)
    factors = [jnp.exp(peak - top) for peak in peaks]
    whole = functools.reduce(jnp.add, [f * t for f, t in zip(factors, totals)])
    attended = None
    for part, factor in zip(parts, factors):
        share = jnp.sum(jnp.where(diagonal, factor / whole, 0.0), axis=1, keepdims=True)
        term = part[:ROWS] * share
        attended = term if attended is None else attended + term
    heads[y, z] = attended.astype(BF16)
    for k in FAR_FIRST[:-1]:
        start(remote(heads.at[y, z], heads.at[y, z], gs.at[k - 1], gr.at[z], at_z(k)))
    load_wo.wait()
    for n in NEAR_FIRST:
        slot = lax.rem(z + n, NZ)
        if n:
            remote(heads.at[y, slot], heads.at[y, slot], gs.at[n - 1], gr.at[slot], at_z(n)).wait_recv()
        for k in (2, 1, 3):
            start(
                remote(
                    heads.at[y, slot], heads.at[y, slot], hs.at[k - 1, slot], hr.at[y, slot], at_y(k)
                )
            )
    for k in (0, 1, 3, 2):
        block = lax.rem(y + k, NY)
        if k:
            for j in range(NZ):
                remote(
                    heads.at[block, j], heads.at[block, j], hs.at[k - 1, j], hr.at[block, j], at_y(k)
                ).wait_recv()
        rows = jnp.swapaxes(heads[block].reshape(NZ * OWN, REP, HD), 0, 1)
        rows = jnp.concatenate([rows[r] for r in range(REP)], axis=1)
        product = jnp.dot(rows, wo[...], preferred_element_type=F32).astype(BF16)
        for half in range(2):
            g = block * 2 + half
            osend[g] = product[16 * half : 16 * (half + 1)]

            @pl.when(g != p)
            def _():
                remote(osend.at[g], orecv.at[p], os_.at[g], or_.at[p], (g, s)).start()

    for dx, dc in others:
        g = prefix_of(dx, dc)
        remote(osend.at[g], orecv.at[g], os_.at[g], or_.at[g], (g, s)).wait_recv()
    result = osend[p].astype(F32)
    for dx, dc in others:
        result = result + orecv[prefix_of(dx, dc)].astype(F32)
    out[...] = result.astype(BF16)

    for copy in pending:
        copy.wait_send()
    for dx, dc in others:
        g = prefix_of(dx, dc)
        remote(osend.at[g], orecv.at[p], os_.at[g], or_.at[p], (g, s)).wait_send()


def on_device(
    hidden_states, query_weight, prefix_levels, prefix_scale, suffix_cache, lengths, output_weight
):
    anywhere = pl.BlockSpec(memory_space=pl.ANY)
    scalar = pl.BlockSpec(memory_space=pltpu.SMEM)
    dma = pltpu.SemaphoreType.DMA
    call = pl.pallas_call(
        kernel,
        out_shape=pltpu.VMEM((16, 256), BF16),
        in_specs=[anywhere] * 7,
        out_specs=pl.BlockSpec(memory_space=pltpu.VMEM),
        scratch_shapes=[
            pltpu.VMEM((128, 256), BF16),
            pltpu.VMEM((256, COLS), BF16),
            pltpu.VMEM((COLS, 256), BF16),
            pltpu.VMEM((2, SPAN * GROUPS, HD), BF16),
            pltpu.VMEM((2, OWN, SPAN * GROUPS, HD), BF16),
            pltpu.VMEM((2, GROUPS, SPAN, HD), BF16),
            pltpu.VMEM((2, OWN, GROUPS, SPAN, HD), BF16),
            pltpu.VMEM((128, WIDE), F32),
            pltpu.VMEM((NY - 1, NZ, OWN, WIDE), BF16),
            pltpu.VMEM((NY - 1, NZ, OWN, WIDE), BF16),
            pltpu.VMEM((NZ, OWN, WIDE), F32),
            pltpu.VMEM((NZ - 1, OWN, WIDE), BF16),
            pltpu.VMEM((NZ - 1, OWN, WIDE), BF16),
            pltpu.VMEM((ROWS, HD), F32),
            pltpu.VMEM((NP, ROWS, HD), BF16),
            pltpu.VMEM((NP, ROWS + 8, HD), F32),
            pltpu.VMEM((NP, ROWS + 8, HD), F32),
            pltpu.VMEM((NY, NZ, ROWS, HD), BF16),
            pltpu.VMEM((NP, 16, 256), BF16),
            pltpu.VMEM((NP, 16, 256), BF16),
            pltpu.SMEM((2, 4, 8), F32),
            pltpu.SMEM((4,), jnp.int32),
            pltpu.SemaphoreType.REGULAR((2,)),
            dma((5,)),
            dma((2, OWN + 1)),
            dma((NY - 1, NZ)),
            dma((NY - 1, NZ)),
            dma((NZ - 1,)),
            dma((NZ - 1,)),
            dma((NP - 1,)),
            dma((NP,)),
            dma((NP,)),
            dma((NP,)),
            dma((NZ - 1,)),
            dma((NZ,)),
            dma((NY - 1, NZ)),
            dma((NY, NZ)),
            dma((NP,)),
            dma((NP,)),
        ],
        compiler_params=pltpu.CompilerParams(
            collective_id=0, has_side_effects=True, vmem_limit_bytes=60 * 2**20
        ),
        name="layer",
    )
    return call(
        prefix_scale,
        lengths,
        hidden_states,
        query_weight,
        prefix_levels.reshape(2, SPAN * GROUPS, HD),
        suffix_cache.reshape(2, OWN, SPAN * GROUPS, HD),
        output_weight,
    )


def solution(mesh):
    return jax.shard_map(
        on_device,
        mesh=mesh,
        in_specs=(
            P(None, "sample"),
            P("sample", "prefix"),
            P(None, "prefix", None, None),
            P(None, "prefix", None),
            P(None, "sample", "prefix", None, None),
            P("sample"),
            P("prefix", "sample"),
        ),
        out_specs=P("prefix", "sample"),
        check_vma=False,
    )
```

```python
import functools
import math

import jax
import jax.numpy as jnp
from jax import lax
from jax.experimental import pallas as pl
from jax.experimental.pallas import tpu as pltpu
from jax.sharding import PartitionSpec as P

MESH = pl.DeviceIdType.MESH
EPSILON = 1e-05
BLOCK = 128
NX, NC, NY, NZ = 4, 2, 4, 8
NP = NX * NC
OWN = 4
HD = 128
GROUPS = 8
REP = 8
ROWS = OWN * REP
COLS = REP * HD
WIDE = COLS + 128
SPAN = 512
D = 8192
SCALING = 1.0 / math.sqrt(HD)
X_ORDER = (0, 1, 3, 2)
TURNS = (((0, 0), (0, 1)), ((1, 0), (1, 1), (3, 0), (3, 1)), ((2, 0), (2, 1)))
PAIRS = (2, 1, 3, 0)
FAR_FIRST = (4, 3, 5, 2, 6, 1, 7, 0)
NEAR_FIRST = FAR_FIRST[::-1]
F32 = jnp.float32
BF16 = jnp.bfloat16


def split_lanes(values):
    folded = values + pltpu.roll(values, 64, 1)
    high = folded.astype(BF16).astype(F32)
    lane = lax.broadcasted_iota(jnp.int32, folded.shape, 1)
    return jnp.where(lane < 64, high, folded - high)


def regroup(source, target):
    tokens = 64

    @pl.loop(0, SPAN // tokens)
    def _(step):
        rows = source[pl.ds(pl.multiple_of(step * tokens * GROUPS, tokens * GROUPS), tokens * GROUPS), :]
        rows = jnp.swapaxes(rows.reshape(tokens, GROUPS, HD), 0, 1)
        target[:, pl.ds(pl.multiple_of(step * tokens, tokens), tokens), :] = rows


def across(a, b):
    return lax.dot_general(a, b, (((1,), (1,)), ((), ())), preferred_element_type=F32)


def kernel(
    scale_hbm, lengths_hbm, hidden_hbm, wq_hbm, prefix_hbm, suffix_hbm, wo_hbm, out,
    hidden, wq, wo, praw, sraw, pre, suf, partial, ysend, yrecv, mine, kept, zsend, zrecv, qrows, qall,
    csend, crecv, heads, osend, orecv,
    scale, lengths, ready, load_sem, raw_sem, ys, yr, zs, zr, qs, qr, cs, cr, gs, gr, hs, hr, os_, or_,
):
    p = lax.axis_index("prefix")
    s = lax.axis_index("sample")
    x, c = p // NC, p % NC
    y, z = s // NZ, s % NZ

    def at_y(k):
        return (p, lax.rem(y + k, NY) * NZ + z)

    def at_z(k):
        return (p, y * NZ + lax.rem(z + k, NZ))

    def prefix_of(dx, dc):
        return lax.rem(x + dx, NX) * NC + lax.rem(c + dc, NC)

    def remote(src, dst, ssem, rsem, device):
        return pltpu.make_async_remote_copy(
            src_ref=src, dst_ref=dst, send_sem=ssem, recv_sem=rsem, device_id=device, device_id_type=MESH
        )

    pending = []

    def start(copy):
        copy.start()
        pending.append(copy)
        return copy

    others = [(dx, dc) for dx in X_ORDER for dc in range(NC) if dx or dc]

    load_hidden = pltpu.make_async_copy(hidden_hbm, hidden, load_sem.at[0])
    load_wq = pltpu.make_async_copy(wq_hbm, wq, load_sem.at[1])
    load_wo = pltpu.make_async_copy(wo_hbm, wo, load_sem.at[2])
    load_scale = pltpu.make_async_copy(scale_hbm, scale, load_sem.at[3])
    load_lengths = pltpu.make_async_copy(lengths_hbm, lengths, load_sem.at[4])
    load_hidden.start()
    load_wq.start()
    load_scale.start()
    load_lengths.start()

    barrier = pltpu.get_barrier_semaphore()
    for k in (1, NZ - 1):
        pl.semaphore_signal(barrier, inc=1, device_id=at_z(k), device_id_type=MESH)
    for k in range(1, NY):
        pl.semaphore_signal(barrier, inc=1, device_id=at_y(k), device_id_type=MESH)
    for dx, dc in others:
        pl.semaphore_signal(barrier, inc=1, device_id=(prefix_of(dx, dc), s), device_id_type=MESH)

    load_hidden.wait()
    load_wq.wait()

    raw = []
    for side in range(2):
        for i in range(OWN):
            raw.append(
                (
                    pltpu.make_async_copy(suffix_hbm.at[side, i], sraw.at[side, i], raw_sem.at[side, i]),
                    sraw.at[side, i],
                    suf.at[side, i // 2, :, :, pl.ds(HD * (i % 2), HD)],
                )
            )
        raw.append(
            (
                pltpu.make_async_copy(prefix_hbm.at[side], praw.at[side], raw_sem.at[side, OWN]),
                praw.at[side],
                pre.at[side],
            )
        )
    for copy, _, _ in raw:
        copy.start()
    load_wo.start()

    wide = 256
    for n in range(COLS // wide):
        cols = pl.ds(n * wide, wide)
        partial[:, cols] = jnp.dot(hidden[...], wq[:, cols], preferred_element_type=F32)
    values = hidden[...].astype(F32)
    values = values * values
    partial[:, COLS:] = split_lanes(values[:, :128] + values[:, 128:])

    pl.semaphore_wait(barrier, 2 + NY - 1 + NP - 1)
    for k in (1, NZ - 1):
        pl.semaphore_signal(ready.at[0], inc=1, device_id=at_z(k), device_id_type=MESH)

    pairs, tall = NZ // 2, 2 * OWN
    for k in range(1, NY):
        first = pl.multiple_of(lax.rem(y + k, NY) * NZ * OWN, NZ * OWN)
        block = partial[pl.ds(first, NZ * OWN), :].astype(BF16)
        for j in range(pairs):
            ysend[k - 1, j] = block[tall * j : tall * (j + 1)]
    ycopies = []
    for m in PAIRS:
        slot = lax.rem(z // 2 + m, pairs)
        for k in (2, 1, 3):
            copy = remote(
                ysend.at[k - 1, slot], yrecv.at[k - 1, m], ys.at[k - 1, m], yr.at[k - 1, m], at_y(k)
            )
            ycopies.append(start(copy))
    first = pl.multiple_of(y * NZ * OWN, NZ * OWN)
    block = partial[pl.ds(first, NZ * OWN), :]
    for j in range(pairs):
        mine[j] = block[tall * j : tall * (j + 1)]

    for n, (copy, source, target) in enumerate(raw[: OWN + 1]):
        copy.wait()
        regroup(source, target)
        if n == 1:
            pl.semaphore_wait(ready.at[0], 2)
            for k in (2, NZ - 2):
                pl.semaphore_signal(ready.at[1], inc=1, device_id=at_z(k), device_id_type=MESH)
    pl.semaphore_wait(ready.at[1], 2)
    for i, m in enumerate(PAIRS):
        slot = lax.rem(z // 2 + m, pairs)
        summed = mine[slot]
        for j, k in enumerate((2, 1, 3)):
            ycopies[(NY - 1) * i + j].wait_recv()
            summed = summed + yrecv[k - 1, m].astype(F32)
        squares = split_lanes(summed[:, COLS:])
        for half in range(2):
            rows = slice(OWN * half, OWN * (half + 1))
            target = slot * 2 + half
            zsend[target, :, :COLS] = summed[rows, :COLS].astype(BF16)
            zsend[target, :, COLS:] = squares[rows].astype(BF16)
            if m:
                start(
                    remote(zsend.at[target], zrecv.at[z], zs.at[target], zr.at[z], (p, y * NZ + target))
                )
            else:
                kept[half] = summed[rows]
    beside = z + 1 - 2 * (z % 2)
    start(remote(zsend.at[beside], zrecv.at[z], zs.at[beside], zr.at[z], (p, y * NZ + beside)))
    for copy, source, target in raw[OWN + 1 :]:
        copy.wait()
        regroup(source, target)
    for k in range(1, NZ):
        slot = lax.rem(z + k, NZ)
        remote(zsend.at[slot], zrecv.at[slot], zs.at[slot], zr.at[slot], at_z(k)).wait_recv()
    own = kept[z % 2]
    for k in range(1, NZ):
        own = own + zrecv[lax.rem(z + k, NZ)].astype(F32)
    mean_sq = jnp.sum(own[:, COLS:], axis=1, keepdims=True) * (1.0 / D)
    scaled = own[:, :COLS] * lax.rsqrt(mean_sq + EPSILON)
    for r in range(REP):
        qrows[OWN * r : OWN * (r + 1), :] = scaled[:, HD * r : HD * (r + 1)]
    qall[p] = jnp.concatenate(
        [qrows[pl.ds(i, REP, stride=OWN), :] for i in range(OWN)], axis=0
    ).astype(BF16)
    for k, (dx, dc) in enumerate(others[::-1]):
        copy = remote(qall.at[p], qall.at[p], qs.at[k], qr.at[p], (prefix_of(dx, dc), s))
        start(copy)

    load_scale.wait()
    load_lengths.wait()
    first_position = p * SPAN
    place = lax.broadcasted_iota(jnp.int32, (REP, SPAN), 1) + first_position
    live = jnp.concatenate([place < lengths[i] for i in range(OWN)], axis=0)
    upper = lax.broadcasted_iota(jnp.int32, (16, HD), 0) < REP
    row_id = lax.broadcasted_iota(jnp.int32, (ROWS, 128), 0)
    lane_id = lax.broadcasted_iota(jnp.int32, (ROWS, 128), 1)
    diagonal = row_id == lane_id
    top_row = lax.broadcasted_iota(jnp.int32, (8, 128), 0) == 0

    def attend(g):
        q = qall[g]
        raw_scores = across(q, pre[0, g])
        prefix_scores = jnp.concatenate(
            [
                raw_scores[:, BLOCK * b : BLOCK * (b + 1)] * (scale[0, b, g] * SCALING)
                for b in range(SPAN // BLOCK)
            ],
            axis=1,
        )
        pieces = []
        for j in range(OWN // 2):
            pair = q[16 * j : 16 * (j + 1)]
            both = jnp.concatenate([jnp.where(upper, pair, 0), jnp.where(upper, 0, pair)], axis=1)
            pieces.append(across(both, suf[0, j, g]))
        suffix_scores = jnp.where(live, jnp.concatenate(pieces, axis=0) * SCALING, -jnp.inf)
        peak = jnp.maximum(
            jnp.max(prefix_scores, axis=1, keepdims=True), jnp.max(suffix_scores, axis=1, keepdims=True)
        )
        prefix_exp = jnp.exp(prefix_scores - peak)
        suffix_exp = jnp.exp(suffix_scores - peak)
        total = jnp.sum(prefix_exp, axis=1, keepdims=True) + jnp.sum(suffix_exp, axis=1, keepdims=True)
        prefix_weights = jnp.concatenate(
            [
                prefix_exp[:, BLOCK * b : BLOCK * (b + 1)] * scale[1, b, g]
                for b in range(SPAN // BLOCK)
            ],
            axis=1,
        ).astype(BF16)
        suffix_weights = suffix_exp.astype(BF16)
        weighted = jnp.dot(prefix_weights, pre[1, g], preferred_element_type=F32)
        pieces = []
        for j in range(OWN // 2):
            pair = suffix_weights[16 * j : 16 * (j + 1)]
            value = jnp.dot(pair, suf[1, j, g], preferred_element_type=F32)
            pieces += [value[:REP, :HD], value[REP:, HD:]]
        csend[g, :ROWS] = weighted + jnp.concatenate(pieces, axis=0)
        peak_row = jnp.sum(jnp.where(diagonal, peak, 0.0), axis=0, keepdims=True)
        total_row = jnp.sum(jnp.where(diagonal, total, 0.0), axis=0, keepdims=True)
        csend[g, ROWS:] = jnp.where(top_row, peak_row, total_row)

    for together in TURNS:
        for dx, dc in together:
            if dx or dc:
                g = prefix_of(dx, dc)
                remote(qall.at[g], qall.at[g], qs.at[0], qr.at[g], (g, s)).wait_recv()
        for dx, dc in together:
            attend(prefix_of(dx, dc))
        for dx, dc in together:
            if dx or dc:
                g = prefix_of(dx, dc)
                start(remote(csend.at[g], crecv.at[p], cs.at[g], cr.at[p], (g, s)))

    for dx, dc in others:
        g = prefix_of(dx, dc)
        remote(csend.at[g], crecv.at[g], cs.at[g], cr.at[g], (g, s)).wait_recv()

    parts = [csend[p]] + [crecv[prefix_of(dx, dc)] for dx, dc in others]
    peaks = [part[ROWS : ROWS + 1] for part in parts]
    totals = [part[ROWS + 1 : ROWS + 2] for part in parts]
    top = functools.reduce(jnp.maximum, peaks)
    factors = [jnp.exp(peak - top) for peak in peaks]
    whole = functools.reduce(jnp.add, [f * t for f, t in zip(factors, totals)])
    attended = None
    for part, factor in zip(parts, factors):
        share = jnp.sum(jnp.where(diagonal, factor / whole, 0.0), axis=1, keepdims=True)
        term = part[:ROWS] * share
        attended = term if attended is None else attended + term
    heads[y, z] = attended.astype(BF16)
    for k in FAR_FIRST[:-1]:
        start(remote(heads.at[y, z], heads.at[y, z], gs.at[k - 1], gr.at[z], at_z(k)))
    load_wo.wait()
    for n in NEAR_FIRST:
        slot = lax.rem(z + n, NZ)
        if n:
            remote(heads.at[y, slot], heads.at[y, slot], gs.at[n - 1], gr.at[slot], at_z(n)).wait_recv()
        for k in (2, 1, 3):
            start(
                remote(
                    heads.at[y, slot], heads.at[y, slot], hs.at[k - 1, slot], hr.at[y, slot], at_y(k)
                )
            )
    for k in (0, 1, 3, 2):
        block = lax.rem(y + k, NY)
        if k:
            for j in range(NZ):
                remote(
                    heads.at[block, j], heads.at[block, j], hs.at[k - 1, j], hr.at[block, j], at_y(k)
                ).wait_recv()
        rows = jnp.swapaxes(heads[block].reshape(NZ * OWN, REP, HD), 0, 1)
        rows = jnp.concatenate([rows[r] for r in range(REP)], axis=1)
        product = jnp.dot(rows, wo[...], preferred_element_type=F32).astype(BF16)
        for half in range(2):
            g = block * 2 + half
            osend[g] = product[16 * half : 16 * (half + 1)]

            @pl.when(g != p)
            def _():
                remote(osend.at[g], orecv.at[p], os_.at[g], or_.at[p], (g, s)).start()

    for dx, dc in others:
        g = prefix_of(dx, dc)
        remote(osend.at[g], orecv.at[g], os_.at[g], or_.at[g], (g, s)).wait_recv()
    result = osend[p].astype(F32)
    for dx, dc in others:
        result = result + orecv[prefix_of(dx, dc)].astype(F32)
    out[...] = result.astype(BF16)

    for copy in pending:
        copy.wait_send()
    for dx, dc in others:
        g = prefix_of(dx, dc)
        remote(osend.at[g], orecv.at[p], os_.at[g], or_.at[p], (g, s)).wait_send()


def on_device(
    hidden_states, query_weight, prefix_levels, prefix_scale, suffix_cache, lengths, output_weight
):
    anywhere = pl.BlockSpec(memory_space=pl.ANY)
    scalar = pl.BlockSpec(memory_space=pltpu.SMEM)
    dma = pltpu.SemaphoreType.DMA
    call = pl.pallas_call(
        kernel,
        out_shape=pltpu.VMEM((16, 256), BF16),
        in_specs=[anywhere] * 7,
        out_specs=pl.BlockSpec(memory_space=pltpu.VMEM),
        scratch_shapes=[
            pltpu.VMEM((128, 256), BF16),
            pltpu.VMEM((256, COLS), BF16),
            pltpu.VMEM((COLS, 256), BF16),
            pltpu.VMEM((2, SPAN * GROUPS, HD), BF16),
            pltpu.VMEM((2, OWN, SPAN * GROUPS, HD), BF16),
            pltpu.VMEM((2, GROUPS, SPAN, HD), BF16),
            pltpu.VMEM((2, OWN // 2, GROUPS, SPAN, 2 * HD), BF16),
            pltpu.VMEM((128, WIDE), F32),
            pltpu.VMEM((NY - 1, NZ // 2, 2 * OWN, WIDE), BF16),
            pltpu.VMEM((NY - 1, NZ // 2, 2 * OWN, WIDE), BF16),
            pltpu.VMEM((NZ // 2, 2 * OWN, WIDE), F32),
            pltpu.VMEM((2, OWN, WIDE), F32),
            pltpu.VMEM((NZ, OWN, WIDE), BF16),
            pltpu.VMEM((NZ, OWN, WIDE), BF16),
            pltpu.VMEM((ROWS, HD), F32),
            pltpu.VMEM((NP, ROWS, HD), BF16),
            pltpu.VMEM((NP, ROWS + 8, HD), F32),
            pltpu.VMEM((NP, ROWS + 8, HD), F32),
            pltpu.VMEM((NY, NZ, ROWS, HD), BF16),
            pltpu.VMEM((NP, 16, 256), BF16),
            pltpu.VMEM((NP, 16, 256), BF16),
            pltpu.SMEM((2, 4, 8), F32),
            pltpu.SMEM((4,), jnp.int32),
            pltpu.SemaphoreType.REGULAR((2,)),
            dma((5,)),
            dma((2, OWN + 1)),
            dma((NY - 1, NZ // 2)),
            dma((NY - 1, NZ // 2)),
            dma((NZ,)),
            dma((NZ,)),
            dma((NP - 1,)),
            dma((NP,)),
            dma((NP,)),
            dma((NP,)),
            dma((NZ - 1,)),
            dma((NZ,)),
            dma((NY - 1, NZ)),
            dma((NY, NZ)),
            dma((NP,)),
            dma((NP,)),
        ],
        compiler_params=pltpu.CompilerParams(
            collective_id=0, has_side_effects=True, vmem_limit_bytes=60 * 2**20
        ),
        name="layer",
    )
    return call(
        prefix_scale,
        lengths,
        hidden_states,
        query_weight,
        prefix_levels.reshape(2, SPAN * GROUPS, HD),
        suffix_cache.reshape(2, OWN, SPAN * GROUPS, HD),
        output_weight,
    )


def solution(mesh):
    return jax.shard_map(
        on_device,
        mesh=mesh,
        in_specs=(
            P(None, "sample"),
            P("sample", "prefix"),
            P(None, "prefix", None, None),
            P(None, "prefix", None),
            P(None, "sample", "prefix", None, None),
            P("sample"),
            P("prefix", "sample"),
        ),
        out_specs=P("prefix", "sample"),
        check_vma=False,
    )
```
